768 devices in a mesh: batch: 16 (over x, y_lo), proto: 48 (over y_hi, z, core).
Axes of the slice: x: 4, y: 8 (y_hi: 2, y_lo: 4; y = y_hi * 4 + y_lo), z: 12, core: 2. Of those that a mesh axis runs over, the one named last changes fastest.
Arguments:
- features: bfloat16 [8192, 256], P('batch'), may hold values from -6 to 6
- prototypes: bfloat16 [98304, 256], P(('proto', 'batch')), may hold values from -6 to 6
Outputs:
- assignments: bfloat16 [8192, 98304], P('batch', 'proto')
The draws below stay inside these ranges and needn't reach their ends.
All inputs are finite; a program needn't handle non-finite values.
Results may differ from the reference program's by a relative error of at most 0.0061.
Values may be sent and summed in bfloat16 or wider, within the bound.
A program may use at most 32 MiB of HBM per device.

```python
import jax
import jax.numpy as jnp
from jax import lax

D = 256
ITERS = 3
B = 8192
K = 98304


def cluster_centres(key):
    return jax.random.truncated_normal(jax.random.fold_in(key, 7), -3.0, 3.0, (16, D), jnp.float32)


def cluster_labels(key, row_total, reverse):
    bounds = jnp.array([303, 454, 555, 631, 692, 742, 785, 823, 857, 887, 915, 940, 963, 985, 1005], jnp.int32)
    ticket = jax.random.randint(key, (row_total,), 0, 1024, jnp.int32)
    labels = jnp.sum((ticket[:, None] >= bounds[None, :]).astype(jnp.int32), axis=1)
    if reverse:
        return 15 - labels
    return labels


def draw_features(key, part):
    centres = cluster_centres(key)
    labels = cluster_labels(jax.random.fold_in(key, 11), B, False)
    noise = jax.random.truncated_normal(jax.random.fold_in(key, 13), -3.0, 3.0, (B, D), jnp.float32)
    strength = 0.58
    return (strength * centres[labels] + noise).astype(jnp.bfloat16)


def draw_prototypes(key, part):
    centres = cluster_centres(key)
    labels = cluster_labels(jax.random.fold_in(key, 17), K, True)
    noise = jax.random.truncated_normal(jax.random.fold_in(key, 19), -3.0, 3.0, (K, D), jnp.float32)
    strength = 0.58
    return (strength * centres[labels] + noise).astype(jnp.bfloat16)


def setup_inputs(seed: int = 0) -> dict:
    key_list = jax.random.split(jax.random.key(seed), 3)
    return {
        "features": draw_features(jax.random.fold_in(key_list[2], 71), 0),
        "prototypes": draw_prototypes(jax.random.fold_in(key_list[2], 71), 0),
    }


def unit_rows(matrix):
    values = matrix.astype(jnp.float32)
    scale = jax.lax.rsqrt(1e-06 + lax.optimization_barrier(jnp.sum(values * values, axis=1, keepdims=True)))
    return (values * scale).astype(jnp.bfloat16)

def reference(features, prototypes):
    unit_feat = unit_rows(features)
    unit_proto = unit_rows(prototypes)
    scores = jnp.dot(unit_feat, unit_proto.T, preferred_element_type=jnp.float32)
    weights = jnp.exp(20.0 * scores)
    for step in range(ITERS):
        weights = weights / lax.optimization_barrier(jnp.sum(weights, axis=0, keepdims=True))
        weights = weights / lax.optimization_barrier(jnp.sum(weights, axis=1, keepdims=True))
    return (float(K) * weights).astype(jnp.bfloat16)
```

```python
import jax
import jax.numpy as jnp
from jax import lax
from jax.experimental import pallas as pl
from jax.experimental.pallas import tpu as pltpu
from jax.sharding import PartitionSpec as P

ITERS = 3
NX, NY, NZ = 4, 4, 12
ROWS, COLS, DEPTH, BLOCK = 512, 2048, 256, 128
TOTAL_PROTOS = 98304.0
MESH = pl.DeviceIdType.MESH
NT = (((1,), (1,)), ((), ()))


def unit_rows(values):
    values = values.astype(jnp.float32)
    scale = lax.rsqrt(1e-06 + jnp.sum(values * values, axis=1, keepdims=True))
    return (values * scale).astype(jnp.bfloat16)


def split(values):
    high = values.astype(jnp.bfloat16)
    low = (values - high.astype(jnp.float32)).astype(jnp.bfloat16)
    return high, low


def kernel(
    feat_ref, proto_ref, scaled_ref, row_ref,
    blocks, unit_feat, weights,
    col_own, col_x, col_y, row_own, row_a, row_z,
    y_send, y_recv, x_send, x_recv, f_send, f_recv,
    cx_send, cx_recv, cy_send, cy_recv, ra_send, ra_recv, rz_send, rz_recv,
):
    batch, proto = lax.axis_index("batch"), lax.axis_index("proto")
    x, y = batch // NY, batch % NY
    yh, z, core = proto // (2 * NZ), (proto // 2) % NZ, proto % 2
    xs = [lax.rem(x + d, NX) for d in range(NX)]
    ys = [y, y + 1 - 2 * lax.rem(y, 2), lax.rem(y + 2, NY), NY - 1 - y]
    near = [(yh, 1 - core), (1 - yh, core), (1 - yh, 1 - core)]
    zs = [lax.rem(z + d, NZ) for d in range(NZ)]

    def at(px, py):
        return {"batch": px * NY + py, "proto": proto}

    def over(pyh, pz, pcore):
        return {"batch": batch, "proto": (pyh * NZ + pz) * 2 + pcore}

    barrier = pltpu.get_barrier_semaphore()
    partners = [at(px, y) for px in xs[1:]] + [at(x, py) for py in ys[1:]]
    partners += [over(a, z, b) for a, b in near] + [over(yh, pz, core) for pz in zs[1:]]
    for partner in partners:
        pl.semaphore_signal(barrier, inc=1, device_id=partner, device_id_type=MESH)
    blocks[batch] = unit_rows(proto_ref[...])
    unit_feat[...] = unit_rows(feat_ref[...])
    pl.semaphore_wait(barrier, len(partners))

    def remote(src, dst, send, recv, device):
        copy = pltpu.make_async_remote_copy(
            src_ref=src, dst_ref=dst, send_sem=send, recv_sem=recv,
            device_id=device, device_id_type=MESH,
        )
        copy.start()
        return copy

    sent = []

    def compute(index):
        scores = lax.dot_general(
            unit_feat[...], blocks[index], NT, preferred_element_type=jnp.float32
        )
        columns = pl.ds(pl.multiple_of(index * BLOCK, BLOCK), BLOCK)
        weights[:, columns] = jnp.exp(20.0 * scores).astype(jnp.bfloat16)

    right, left, across = xs[1], xs[3], xs[2]
    half = BLOCK // 2
    x_copies, f_copies = {}, {}

    def spread(k):
        block = blocks.at[x * NY + ys[k]]
        x_copies[k] = [
            remote(block, block, x_send.at[k, 0], x_recv.at[k, 0], at(right, y)),
            remote(block, block, x_send.at[k, 1], x_recv.at[k, 1], at(left, y)),
        ]
        sent.extend(x_copies[k])

    def forward(k):
        x_copies[k][0].wait_recv()
        block = blocks.at[left * NY + ys[k], pl.ds(0, half)]
        first = remote(block, block, f_send.at[k, 0], f_recv.at[k, 0], at(right, y))
        x_copies[k][1].wait_recv()
        block = blocks.at[right * NY + ys[k], pl.ds(half, half)]
        second = remote(block, block, f_send.at[k, 1], f_recv.at[k, 1], at(left, y))
        f_copies[k] = [first, second]
        sent.extend(f_copies[k])
        compute(left * NY + ys[k])
        compute(right * NY + ys[k])

    def finish(k):
        for copy in f_copies[k]:
            copy.wait_recv()
        compute(across * NY + ys[k])

    spread(0)
    own = blocks.at[batch]
    y_copies = [
        remote(own, own, y_send.at[k - 1], y_recv.at[k - 1], at(x, ys[k])) for k in range(1, NY)
    ]
    sent.extend(y_copies)
    compute(batch)
    for k in range(1, NY):
        y_copies[k - 1].wait_recv()
        spread(k)
        forward(k - 1)
        compute(x * NY + ys[k])
        if k > 1:
            finish(k - 2)
    forward(NY - 1)
    finish(NY - 2)
    finish(NY - 1)

    col_mask = lax.broadcasted_iota(jnp.int32, (8, COLS), 1) // 256 == lax.broadcasted_iota(
        jnp.int32, (8, COLS), 0
    )
    row_of = lax.broadcasted_iota(jnp.int32, (8, 256), 0)
    row_factor = [jnp.ones((1, BLOCK), jnp.float32)] * 4
    for step in range(ITERS):
        wide = jnp.concatenate([jnp.broadcast_to(part, (8, BLOCK)) for part in row_factor], axis=1)
        if step:
            high, low = split(wide)
            summed = jnp.dot(high, weights[...], preferred_element_type=jnp.float32)
            summed += jnp.dot(low, weights[...], preferred_element_type=jnp.float32)
        else:
            summed = jnp.dot(
                wide.astype(jnp.bfloat16), weights[...], preferred_element_type=jnp.float32
            )
        part = jnp.zeros((8, 256), jnp.float32)
        for k in range(8):
            part = jnp.where(row_of == k, summed[:, k * 256:(k + 1) * 256], part)

        def exchange(value, mine, slots, send, recv, devices):
            mine[...] = value
            copies = [
                remote(mine, slots.at[i], send.at[i], recv.at[i], device)
                for i, device in enumerate(devices)
            ]
            sent.extend(copies)
            total = value
            for i, copy in enumerate(copies):
                copy.wait_recv()
                total = total + slots[i]
            return total

        part = exchange(
            part, col_own.at[step, 0], col_x.at[step], cx_send.at[step], cx_recv.at[step],
            [at(px, y) for px in xs[1:]],
        )
        part = exchange(
            part, col_own.at[step, 1], col_y.at[step], cy_send.at[step], cy_recv.at[step],
            [at(x, py) for py in ys[1:]],
        )
        col_factor = 1.0 / part
        tiled = jnp.where(col_mask, jnp.concatenate([col_factor] * 8, axis=1), 0.0)
        high, low = split(tiled)
        rows = lax.dot_general(high, weights[...], NT, preferred_element_type=jnp.float32)
        rows += lax.dot_general(low, weights[...], NT, preferred_element_type=jnp.float32)
        rows = jnp.sum(rows, axis=0, keepdims=True)
        part = jnp.concatenate([rows[:, k * BLOCK:(k + 1) * BLOCK] for k in range(4)], axis=0)
        part = exchange(
            part, row_own.at[step, 0], row_a.at[step], ra_send.at[step], ra_recv.at[step],
            [over(a, z, b) for a, b in near],
        )
        if step == ITERS - 1:
            flat = jnp.sum(tiled, axis=0, keepdims=True) * TOTAL_PROTOS
            scaled_ref[...] = (weights[...].astype(jnp.float32) * flat).astype(jnp.bfloat16)
        part = exchange(
            part, row_own.at[step, 1], row_z.at[step], rz_send.at[step], rz_recv.at[step],
            [over(yh, pz, core) for pz in zs[1:]],
        )
        result = 1.0 / part
        row_factor = [result[k:k + 1] for k in range(4)]
    row_ref[...] = result
    for copy in sent:
        copy.wait_send()


def local(features, prototypes):
    vmem = pl.BlockSpec(memory_space=pltpu.VMEM)
    dma = pltpu.SemaphoreType.DMA
    scaled, rows = pl.pallas_call(
        kernel,
        out_shape=(
            jax.ShapeDtypeStruct((ROWS, COLS), jnp.bfloat16),
            jax.ShapeDtypeStruct((4, BLOCK), jnp.float32),
        ),
        in_specs=[vmem, vmem],
        out_specs=(vmem, vmem),
        scratch_shapes=[
            pltpu.VMEM((NX * NY, BLOCK, DEPTH), jnp.bfloat16),
            pltpu.VMEM((ROWS, DEPTH), jnp.bfloat16),
            pltpu.VMEM((ROWS, COLS), jnp.bfloat16),
            pltpu.VMEM((ITERS, 2, 8, 256), jnp.float32),
            pltpu.VMEM((ITERS, 3, 8, 256), jnp.float32),
            pltpu.VMEM((ITERS, 3, 8, 256), jnp.float32),
            pltpu.VMEM((ITERS, 2, 4, BLOCK), jnp.float32),
            pltpu.VMEM((ITERS, 3, 4, BLOCK), jnp.float32),
            pltpu.VMEM((ITERS, NZ - 1, 4, BLOCK), jnp.float32),
            dma((3,)), dma((3,)), dma((4, 2)), dma((4, 2)), dma((4, 2)), dma((4, 2)),
            dma((ITERS, 3)), dma((ITERS, 3)), dma((ITERS, 3)), dma((ITERS, 3)),
            dma((ITERS, 3)), dma((ITERS, 3)), dma((ITERS, NZ - 1)), dma((ITERS, NZ - 1)),
        ],
        compiler_params=pltpu.CompilerParams(collective_id=0, has_side_effects=True),
    )(features, prototypes)
    return (scaled.astype(jnp.float32) * rows.reshape(ROWS)[:, None]).astype(jnp.bfloat16)


def solution(mesh):
    in_specs = (P("batch", None), P(("proto", "batch"), None))
    out_specs = P("batch", "proto")
    return jax.shard_map(local, mesh=mesh, in_specs=in_specs, out_specs=out_specs, check_vma=False)
```

```python
import jax
import jax.numpy as jnp
from jax import lax
from jax.experimental import pallas as pl
from jax.experimental.pallas import tpu as pltpu
from jax.sharding import PartitionSpec as P

ITERS = 3
NX, NY, NZ, RING = 4, 4, 12, 8
ROWS, COLS, DEPTH, BLOCK = 512, 2048, 256, 128
TILE, HALF = 1024, 256
TOTAL_PROTOS = 98304.0
MESH = pl.DeviceIdType.MESH
NT = (((1,), (1,)), ((), ()))
F32, BF16 = jnp.float32, jnp.bfloat16


def unit_rows(values):
    values = values.astype(F32)
    scale = lax.rsqrt(1e-06 + jnp.sum(values * values, axis=1, keepdims=True))
    return (values * scale).astype(BF16)


def split(values):
    high = values.astype(BF16)
    low = (values - high.astype(F32)).astype(BF16)
    return jnp.concatenate([high, low], axis=0)


def kernel(
    feat_ref, proto_ref, scaled_ref, row_ref,
    own_feat, feats, protos, other, weights,
    col_own, col_in, ring_own, ring_in, z_own, z_in, last_own, last_in, lastz_own, lastz_in, col_last,
    fs, fr, ps, pr, gs, gr, cs, cr, ys, yr, zs, zr, ls, lr, lzs, lzr, bs, br, es, er, hs, hr, ks, kr,
):
    batch, proto = lax.axis_index("batch"), lax.axis_index("proto")
    x, yl = batch // NY, lax.rem(batch, NY)
    yh, z, core = proto // (2 * NZ), lax.rem(proto // 2, NZ), lax.rem(proto, 2)
    y = yh * NY + yl
    mate = 1 - core

    def device(px, py, pz, pcore):
        return {
            "batch": px * NY + lax.rem(py, NY),
            "proto": ((py // NY) * NZ + pz) * 2 + pcore,
        }

    xs = [lax.rem(x + d, NX) for d in range(NX)]
    ry = [lax.rem(y + d, RING) for d in range(RING)]
    rz = [lax.rem(z + d, NZ) for d in range(NZ)]
    near_y = [yl, yl + 1 - 2 * lax.rem(yl, 2), lax.rem(yl + 2, NY), NY - 1 - yl]
    col_peers = [device(px, y, z, core) for px in xs[1:]] + [device(px, y, z, mate) for px in xs]
    ring_peers = [device(x, py, z, core) for py in ry[1:]]
    last_peers = [(py, device(x, py, z, core)) for py in ry[1:]]
    last_peers += [(py, device(x, py, z, mate)) for py in ry]
    z_peers = [device(x, y, pz, core) for pz in rz[1:]]

    barrier = pltpu.get_barrier_semaphore()
    partners = col_peers + [peer for _, peer in last_peers if peer is not last_peers[7][1]] + z_peers
    for partner in partners:
        pl.semaphore_signal(barrier, inc=1, device_id=partner, device_id_type=MESH)
    protos[batch] = unit_rows(proto_ref[...])
    own_feat[...] = unit_rows(feat_ref[...])
    mine = pl.ds(pl.multiple_of(core * HALF, HALF), HALF)
    feats[yl] = own_feat[mine, :]
    pl.semaphore_wait(barrier, len(partners))

    sent = []

    def remote(src, dst, send, recv, peer):
        copy = pltpu.make_async_remote_copy(
            src_ref=src, dst_ref=dst, send_sem=send, recv_sem=recv,
            device_id=peer, device_id_type=MESH,
        )
        copy.start()
        sent.append(copy)
        return copy

    block = protos.at[batch]
    proto_copies = [
        remote(block, block, ps.at[d - 1], pr.at[d - 1], device(xs[d], y, z, core)) for d in (1, 3, 2)
    ]
    feat_copies = [
        remote(own_feat.at[mine], feats.at[yl], fs.at[0], fr.at[0], device(x, ry[1], z, core)),
        remote(own_feat.at[mine], feats.at[yl], fs.at[1], fr.at[1], device(x, ry[7], z, core)),
    ]
    for i, py in enumerate((ry[2], ry[6])):
        src = own_feat.at[pl.ds(pl.multiple_of(core * HALF + i * BLOCK, BLOCK), BLOCK)]
        dst = feats.at[yl, pl.ds(i * BLOCK, BLOCK)]
        feat_copies.append(remote(src, dst, fs.at[2 + i], fr.at[2 + i], device(x, py, z, core)))
    partner = device(x, y, z, mate)
    mate_copies = [remote(block, other.at[x], gs.at[0], gr.at[0], partner)]

    def fill(row_block, columns, image, vectors, count):
        scores = lax.dot_general(image, vectors, NT, preferred_element_type=F32)
        rows = pl.ds(pl.multiple_of(row_block * BLOCK, BLOCK), count)
        weights[rows, pl.ds(pl.multiple_of(columns * BLOCK, BLOCK), BLOCK)] = jnp.exp(
            20.0 * scores
        ).astype(BF16)

    def fill_images(row_block, image, count):
        for px in range(NX):
            fill(row_block, core * NX + px, image, protos[px * NY + yl], count)
            fill(row_block, mate * NX + px, image, other[px], count)

    for slot, (copy, d) in enumerate(zip(proto_copies, (3, 1, 2))):
        copy.wait_recv()
        arrived = protos.at[xs[d] * NY + yl]
        mate_copies.append(
            remote(arrived, other.at[xs[d]], gs.at[1 + slot], gr.at[1 + slot], partner)
        )
    for copy in mate_copies:
        copy.wait_recv()
    fill_images(yl * 2, feats[yl], HALF)
    for copy, shift in zip(feat_copies[:2], (3, 1)):
        copy.wait_recv()
        source = lax.rem(yl + shift, NY)
        fill_images(source * 2, feats[source], HALF)
    source = lax.rem(yl + 2, NY)
    for i, copy in enumerate(feat_copies[2:]):
        copy.wait_recv()
        fill_images(source * 2 + i, feats[source, i * BLOCK:(i + 1) * BLOCK], BLOCK)

    tile_mask = lax.broadcasted_iota(jnp.int32, (8, TILE), 1) // BLOCK == lax.broadcasted_iota(
        jnp.int32, (8, TILE), 0
    )
    row_of = lax.broadcasted_iota(jnp.int32, (8, BLOCK), 0)

    def fold(wide):
        part = wide[:, :BLOCK]
        for k in range(1, 8):
            part = jnp.where(row_of == k, wide[:, k * BLOCK:(k + 1) * BLOCK], part)
        return part

    def column_sums(factor):
        wide = jnp.concatenate(
            [jnp.broadcast_to(factor[k:k + 1], (8, BLOCK)) for k in range(8)], axis=1
        )
        summed = jnp.dot(split(wide), weights[...], preferred_element_type=F32)
        return fold(summed[:8] + summed[8:])

    def row_sums(factor):
        wide = jnp.where(tile_mask, jnp.concatenate([factor] * 8, axis=1), 0.0)
        summed = lax.dot_general(split(wide), weights[...], NT, preferred_element_type=F32)
        return fold(jnp.broadcast_to(jnp.sum(summed, axis=0, keepdims=True), (8, TILE)))

    def start(value, own, slots, send, recv, peers):
        own[...] = value.astype(own.dtype)
        return [remote(own, slots.at[i], send.at[i], recv.at[i], peer) for i, peer in enumerate(peers)]

    def finish(total, slots, copies):
        for i, copy in enumerate(copies):
            copy.wait_recv()
            total = total + slots[i].astype(F32)
        return total

    half = BLOCK // 2
    row_factor = jnp.ones((8, BLOCK), F32)
    for step in range(ITERS):
        part = column_sums(row_factor)
        copies = start(part, col_own.at[step], col_in.at[step], cs.at[step], cr.at[step], col_peers)
        part = finish(part, col_in.at[step], copies)
        col_factor = 1.0 / part
        if step == 1:
            for copy in y_copies:
                copy.wait_recv()
            x_copies = []
            for k in range(1, NY):
                block = protos.at[x * NY + near_y[k]]
                for side, d in enumerate((1, 3)):
                    x_copies.append(
                        remote(block, block, es.at[k - 1, side], er.at[k - 1, side], device(xs[d], y, z, core))
                    )
        part = row_sums(col_factor)
        if step == ITERS - 1:
            last_col = jnp.where(core == 0, col_factor[:4], col_factor[4:]) * TOTAL_PROTOS
            col_last[yl] = last_col
            for k in range(4):
                last_own[k] = part[2 * k:2 * k + 2]
            copies = [
                remote(last_own.at[lax.rem(py, NY)], last_in.at[i], ls.at[i], lr.at[i], peer)
                for i, (py, peer) in enumerate(last_peers)
            ]
            k_copies = [
                remote(col_last.at[yl], col_last.at[yl], ks.at[k - 1], kr.at[k - 1],
                       device(x, yh * NY + near_y[k], z, core))
                for k in range(1, NY)
            ]
            mine_sum = last_own[yl]
            mate_sum = jnp.zeros((2, BLOCK), F32)
            for i, copy in enumerate(copies):
                copy.wait_recv()
                if i < 7:
                    mine_sum = mine_sum + last_in[i]
                else:
                    mate_sum = mate_sum + last_in[i]
            first = jnp.where(core == 0, mine_sum, mate_sum)
            second = jnp.where(core == 0, mate_sum, mine_sum)
            part = jnp.concatenate([first, second], axis=0)
            copies = start(part, lastz_own, lastz_in, lzs, lzr, z_peers)
            for copy in f_copies:
                copy.wait_recv()
            for copy in k_copies:
                copy.wait_recv()
            for b in range(NX * NY):
                scores = lax.dot_general(own_feat[...], protos[b], NT, preferred_element_type=F32)
                factor = col_last[b % NY, b // NY:b // NY + 1, :]
                scaled_ref[:, b * BLOCK:(b + 1) * BLOCK] = jnp.exp(20.0 * scores) * factor
            row_ref[...] = 1.0 / finish(part, lastz_in, copies)
            break
        copies = start(part, ring_own.at[step], ring_in.at[step], ys.at[step], yr.at[step], ring_peers)
        part = finish(part, ring_in.at[step], copies)
        copies = start(part, z_own.at[step], z_in.at[step], zs.at[step], zr.at[step], z_peers)
        if step == 0:
            block = protos.at[batch]
            y_copies = [
                remote(block, block, bs.at[k - 1], br.at[k - 1], device(x, yh * NY + near_y[k], z, core))
                for k in range(1, NY)
            ]
        else:
            f_copies = []
            for k in range(1, NY):
                for side, (source, d) in enumerate(((xs[3], 1), (xs[1], 3))):
                    x_copies[2 * (k - 1) + side].wait_recv()
                    piece = protos.at[source * NY + near_y[k], pl.ds(side * half, half)]
                    f_copies.append(
                        remote(piece, piece, hs.at[k - 1, side], hr.at[k - 1, side], device(xs[d], y, z, core))
                    )
        row_factor = 1.0 / finish(part, z_in.at[step], copies)
    for copy in sent:
        copy.wait_send()


def local(features, prototypes):
    vmem = pl.BlockSpec(memory_space=pltpu.VMEM)
    dma = pltpu.SemaphoreType.DMA
    early = ITERS - 1
    scaled, rows = pl.pallas_call(
        kernel,
        out_shape=(
            jax.ShapeDtypeStruct((ROWS, COLS), F32),
            jax.ShapeDtypeStruct((4, BLOCK), F32),
        ),
        in_specs=[vmem, vmem],
        out_specs=(vmem, vmem),
        scratch_shapes=[
            pltpu.VMEM((ROWS, DEPTH), BF16),
            pltpu.VMEM((NY, HALF, DEPTH), BF16),
            pltpu.VMEM((NX * NY, BLOCK, DEPTH), BF16),
            pltpu.VMEM((NX, BLOCK, DEPTH), BF16),
            pltpu.VMEM((TILE, TILE), BF16),
            pltpu.VMEM((ITERS, 8, BLOCK), BF16),
            pltpu.VMEM((ITERS, 7, 8, BLOCK), BF16),
            pltpu.VMEM((early, 8, BLOCK), BF16),
            pltpu.VMEM((early, 7, 8, BLOCK), BF16),
            pltpu.VMEM((early, 8, BLOCK), BF16),
            pltpu.VMEM((early, 11, 8, BLOCK), BF16),
            pltpu.VMEM((NY, 2, BLOCK), F32),
            pltpu.VMEM((15, 2, BLOCK), F32),
            pltpu.VMEM((4, BLOCK), F32),
            pltpu.VMEM((11, 4, BLOCK), F32),
            pltpu.VMEM((NY, NX, BLOCK), F32),
            dma((4,)), dma((4,)), dma((3,)), dma((3,)), dma((4,)), dma((4,)),
            dma((ITERS, 7)), dma((ITERS, 7)), dma((early, 7)), dma((early, 7)),
            dma((early, 11)), dma((early, 11)), dma((15,)), dma((15,)), dma((11,)), dma((11,)),
            dma((3,)), dma((3,)), dma((3, 2)), dma((3, 2)), dma((3, 2)), dma((3, 2)), dma((3,)), dma((3,)),
        ],
        compiler_params=pltpu.CompilerParams(
            collective_id=0, has_side_effects=True, vmem_limit_bytes=24 << 20
        ),
    )(features, prototypes)
    return (scaled * rows.reshape(ROWS)[:, None]).astype(BF16)


def solution(mesh):
    in_specs = (P("batch", None), P(("proto", "batch"), None))
    out_specs = P("batch", "proto")
    return jax.shard_map(local, mesh=mesh, in_specs=in_specs, out_specs=out_specs, check_vma=False)
```

```python
import jax
import jax.numpy as jnp
from jax import lax
from jax.experimental import pallas as pl
from jax.experimental.pallas import tpu as pltpu
from jax.sharding import PartitionSpec as P

ITERS = 3
NX, NY, NZ, RING = 4, 4, 12, 8
ROWS, COLS, DEPTH, BLOCK = 512, 2048, 256, 128
TILE, HALF = 1024, 256
TOTAL_PROTOS = 98304.0
MESH = pl.DeviceIdType.MESH
NT = (((1,), (1,)), ((), ()))
F32, BF16 = jnp.float32, jnp.bfloat16


def unit_rows(values):
    values = values.astype(F32)
    scale = lax.rsqrt(1e-06 + jnp.sum(values * values, axis=1, keepdims=True))
    return (values * scale).astype(BF16)


def split(values):
    high = values.astype(BF16)
    low = (values - high.astype(F32)).astype(BF16)
    return jnp.concatenate([high, low], axis=0)


def kernel(
    feat_ref, proto_ref, scaled_ref, row_ref,
    loaded, own_feat, feats, unit_feats, protos, other, unit_protos, weights, across,
    col_own, col_in, ring_own, ring_in, z_own, z_in, last_own, last_in, lastz_own, lastz_in, col_last,
    fs, fr, ps, pr, gs, gr, cs, cr, ys, yr, zs, zr, ls, lr, lzs, lzr, bs, br, es, er, hs, hr, ks, kr, ms, token_a, token_b,
):
    batch, proto = lax.axis_index("batch"), lax.axis_index("proto")
    x, yl = batch // NY, lax.rem(batch, NY)
    yh, z, core = proto // (2 * NZ), lax.rem(proto // 2, NZ), lax.rem(proto, 2)
    y = yh * NY + yl
    mate = 1 - core

    def device(px, py, pz, pcore):
        return {
            "batch": px * NY + lax.rem(py, NY),
            "proto": ((py // NY) * NZ + pz) * 2 + pcore,
        }

    xs = [lax.rem(x + d, NX) for d in range(NX)]
    ry = [lax.rem(y + d, RING) for d in range(RING)]
    rz = [lax.rem(z + d, NZ) for d in range(NZ)]
    near_y = [yl, yl + 1 - 2 * lax.rem(yl, 2), lax.rem(yl + 2, NY), NY - 1 - yl]
    col_peers = [device(xs[d], y, z, c) for d in (2, 1, 3) for c in (core, mate)]
    col_peers.append(device(x, y, z, mate))
    far_y = [ry[d] for d in (4, 3, 5, 2, 6, 1, 7)]
    ring_peers = [device(x, py, z, core) for py in far_y]
    last_peers = [(py, device(x, py, z, core)) for py in far_y]
    last_peers += [(py, device(x, py, z, mate)) for py in far_y + [y]]
    z_peers = [device(x, y, rz[d], core) for d in (6, 5, 7, 4, 8, 3, 9, 2, 10, 1, 11)]

    def signal(semaphore, peers):
        for peer in peers:
            pl.semaphore_signal(semaphore, inc=1, device_id=peer, device_id_type=MESH)

    two_y = [device(x, py, z, core) for py in (ry[2], ry[6])]
    one_y = [device(x, py, z, core) for py in (ry[1], ry[7])]
    two_z = [device(x, y, pz, core) for pz in (rz[2], rz[10])]
    one_z = [device(x, y, pz, core) for pz in (rz[1], rz[11])]
    barrier = pltpu.get_barrier_semaphore()
    partners = two_y + two_z + col_peers + one_y + one_z
    signal(barrier, partners)
    loads = [
        pltpu.make_async_copy(feat_ref, loaded, ms.at[0]),
        pltpu.make_async_copy(proto_ref, protos.at[batch], ms.at[1]),
    ]
    for load in loads:
        load.start()
    pl.semaphore_wait(barrier, len(partners))

    sent = []

    def remote(src, dst, send, recv, peer):
        copy = pltpu.make_async_remote_copy(
            src_ref=src, dst_ref=dst, send_sem=send, recv_sem=recv,
            device_id=peer, device_id_type=MESH,
        )
        copy.start()
        sent.append(copy)
        return copy

    proto_copies = [
        remote(proto_ref, protos.at[batch], ps.at[d - 1], pr.at[d - 1], device(xs[d], y, z, core))
        for d in (2, 1, 3)
    ]
    mine = pl.ds(pl.multiple_of(core * HALF, HALF), HALF)
    feat_copies = [
        remote(feat_ref.at[mine], feats.at[yl], fs.at[i], fr.at[i], peer)
        for i, peer in enumerate(one_y)
    ]
    for i, peer in enumerate(two_y):
        src = feat_ref.at[pl.ds(pl.multiple_of(core * HALF + i * BLOCK, BLOCK), BLOCK)]
        dst = feats.at[yl, pl.ds(i * BLOCK, BLOCK)]
        feat_copies.append(remote(src, dst, fs.at[2 + i], fr.at[2 + i], peer))
    partner = device(x, y, z, mate)
    mate_copies = [remote(proto_ref, other.at[x], gs.at[0], gr.at[0], partner)]
    signal(token_a, two_y + two_z + one_y)

    def place(ref, block, values):
        ref[pl.ds(pl.multiple_of(block * BLOCK, BLOCK), values.shape[0]), :] = values

    def fill(block, count):
        rows = pl.ds(pl.multiple_of(block * BLOCK, BLOCK), count)
        for k in range(0, TILE, HALF):
            scores = lax.dot_general(
                unit_feats[rows, :], unit_protos[k:k + HALF, :], NT, preferred_element_type=F32
            )
            weights[rows, k:k + HALF] = jnp.exp(20.0 * scores).astype(BF16)

    loads[0].wait()
    own_feat[...] = unit_rows(loaded[...])
    place(unit_feats, yl * 2, own_feat[mine, :])
    loads[1].wait()
    place(unit_protos, core * NX + x, unit_rows(protos[batch]))
    for slot, d in ((1, 3), (2, 1), (0, 2)):
        proto_copies[slot].wait_recv()
        arrived = protos.at[xs[d] * NY + yl]
        mate_copies.append(
            remote(arrived, other.at[xs[d]], gs.at[len(mate_copies)], gr.at[len(mate_copies)], partner)
        )
        place(unit_protos, core * NX + xs[d], unit_rows(arrived[...]))
    pl.semaphore_wait(token_a, 6)
    signal(token_b, two_y + two_z)
    for copy, px in zip(mate_copies, (x, xs[3], xs[1], xs[2])):
        copy.wait_recv()
        place(unit_protos, mate * NX + px, unit_rows(other[px]))
    fill(yl * 2, HALF)
    for copy, shift in zip(feat_copies[:2], (3, 1)):
        copy.wait_recv()
        source = lax.rem(yl + shift, NY)
        place(unit_feats, source * 2, unit_rows(feats[source]))
        fill(source * 2, HALF)
    source = lax.rem(yl + 2, NY)
    for i, copy in enumerate(feat_copies[2:]):
        copy.wait_recv()
        place(unit_feats, source * 2 + i, unit_rows(feats[source, i * BLOCK:(i + 1) * BLOCK]))
        fill(source * 2 + i, BLOCK)

    tile_mask = lax.broadcasted_iota(jnp.int32, (8, TILE), 1) // BLOCK == lax.broadcasted_iota(
        jnp.int32, (8, TILE), 0
    )
    row_of = lax.broadcasted_iota(jnp.int32, (8, BLOCK), 0)

    def fold(wide):
        part = wide[:, :BLOCK]
        for k in range(1, 8):
            part = jnp.where(row_of == k, wide[:, k * BLOCK:(k + 1) * BLOCK], part)
        return part

    def column_sums(factor):
        wide = jnp.concatenate(
            [jnp.broadcast_to(factor[k:k + 1], (8, BLOCK)) for k in range(8)], axis=1
        )
        summed = jnp.dot(split(wide), weights[...], preferred_element_type=F32)
        return fold(summed[:8] + summed[8:])

    def row_sums(factor):
        wide = jnp.where(tile_mask, jnp.concatenate([factor] * 8, axis=1), 0.0)
        summed = jnp.dot(split(wide), across[...], preferred_element_type=F32)
        return fold(jnp.broadcast_to(jnp.sum(summed, axis=0, keepdims=True), (8, TILE)))

    def start(value, own, slots, send, recv, peers):
        own[...] = value.astype(own.dtype)
        return [remote(own, slots.at[i], send.at[i], recv.at[i], peer) for i, peer in enumerate(peers)]

    def finish(total, slots, copies):
        for i, copy in enumerate(copies):
            copy.wait_recv()
            total = total + slots[i].astype(F32)
        return total

    half = BLOCK // 2
    row_factor = jnp.ones((8, BLOCK), F32)
    for step in range(ITERS):
        part = column_sums(row_factor)
        copies = start(part, col_own.at[step], col_in.at[step], cs.at[step], cr.at[step], col_peers)
        if step == 0:
            for k in range(0, TILE, HALF):
                for j in range(0, TILE, HALF):
                    scores = lax.dot_general(
                        unit_protos[k:k + HALF, :], unit_feats[j:j + HALF, :], NT,
                        preferred_element_type=F32,
                    )
                    across[k:k + HALF, j:j + HALF] = jnp.exp(20.0 * scores).astype(BF16)
            pl.semaphore_wait(token_b, 4)
        part = finish(part, col_in.at[step], copies)
        col_factor = 1.0 / part
        if step == 1:
            for copy in y_copies:
                copy.wait_recv()
            x_copies = []
            for k in range(1, NY):
                block = protos.at[x * NY + near_y[k]]
                for side, d in enumerate((1, 3)):
                    x_copies.append(
                        remote(block, block, es.at[k - 1, side], er.at[k - 1, side], device(xs[d], y, z, core))
                    )
        part = row_sums(col_factor)
        if step == ITERS - 1:
            last_col = jnp.where(core == 0, col_factor[:4], col_factor[4:]) * TOTAL_PROTOS
            col_last[yl] = last_col
            for k in range(4):
                last_own[k] = part[2 * k:2 * k + 2]
            copies = [
                remote(last_own.at[lax.rem(py, NY)], last_in.at[i], ls.at[i], lr.at[i], peer)
                for i, (py, peer) in enumerate(last_peers)
            ]
            k_copies = [
                remote(col_last.at[yl], col_last.at[yl], ks.at[k - 1], kr.at[k - 1],
                       device(x, yh * NY + near_y[k], z, core))
                for k in range(1, NY)
            ]
            mine_sum = last_own[yl]
            mate_sum = jnp.zeros((2, BLOCK), F32)
            for i, copy in enumerate(copies):
                copy.wait_recv()
                if i < 7:
                    mine_sum = mine_sum + last_in[i]
                else:
                    mate_sum = mate_sum + last_in[i]
            first = jnp.where(core == 0, mine_sum, mate_sum)
            second = jnp.where(core == 0, mate_sum, mine_sum)
            part = jnp.concatenate([first, second], axis=0)
            copies = start(part, lastz_own, lastz_in, lzs, lzr, z_peers)
            for copy in f_copies:
                copy.wait_recv()
            for copy in k_copies:
                copy.wait_recv()
            for b in range(NX * NY):
                scores = lax.dot_general(
                    own_feat[...], unit_rows(protos[b]), NT, preferred_element_type=F32
                )
                factor = col_last[b % NY, b // NY:b // NY + 1, :]
                scaled_ref[:, b * BLOCK:(b + 1) * BLOCK] = jnp.exp(20.0 * scores) * factor
            row_ref[...] = 1.0 / finish(part, lastz_in, copies)
            break
        copies = start(part, ring_own.at[step], ring_in.at[step], ys.at[step], yr.at[step], ring_peers)
        part = finish(part, ring_in.at[step], copies)
        copies = start(part, z_own.at[step], z_in.at[step], zs.at[step], zr.at[step], z_peers)
        if step == 0:
            block = protos.at[batch]
            y_copies = [
                remote(block, block, bs.at[k - 1], br.at[k - 1], device(x, yh * NY + near_y[k], z, core))
                for k in range(1, NY)
            ]
        else:
            f_copies = []
            for k in range(1, NY):
                for side, (source, d) in enumerate(((xs[3], 1), (xs[1], 3))):
                    x_copies[2 * (k - 1) + side].wait_recv()
                    piece = protos.at[source * NY + near_y[k], pl.ds(side * half, half)]
                    f_copies.append(
                        remote(piece, piece, hs.at[k - 1, side], hr.at[k - 1, side], device(xs[d], y, z, core))
                    )
        row_factor = 1.0 / finish(part, z_in.at[step], copies)
    for copy in sent:
        copy.wait_send()


def local(features, prototypes):
    vmem = pl.BlockSpec(memory_space=pltpu.VMEM)
    hbm = pl.BlockSpec(memory_space=pltpu.HBM)
    dma = pltpu.SemaphoreType.DMA
    early = ITERS - 1
    scaled, rows = pl.pallas_call(
        kernel,
        out_shape=(
            jax.ShapeDtypeStruct((ROWS, COLS), F32),
            jax.ShapeDtypeStruct((4, BLOCK), F32),
        ),
        in_specs=[hbm, hbm],
        out_specs=(vmem, vmem),
        scratch_shapes=[
            pltpu.VMEM((ROWS, DEPTH), BF16),
            pltpu.VMEM((ROWS, DEPTH), BF16),
            pltpu.VMEM((NY, HALF, DEPTH), BF16),
            pltpu.VMEM((TILE, DEPTH), BF16),
            pltpu.VMEM((NX * NY, BLOCK, DEPTH), BF16),
            pltpu.VMEM((NX, BLOCK, DEPTH), BF16),
            pltpu.VMEM((TILE, DEPTH), BF16),
            pltpu.VMEM((TILE, TILE), BF16),
            pltpu.VMEM((TILE, TILE), BF16),
            pltpu.VMEM((ITERS, 8, BLOCK), BF16),
            pltpu.VMEM((ITERS, 7, 8, BLOCK), BF16),
            pltpu.VMEM((early, 8, BLOCK), BF16),
            pltpu.VMEM((early, 7, 8, BLOCK), BF16),
            pltpu.VMEM((early, 8, BLOCK), BF16),
            pltpu.VMEM((early, 11, 8, BLOCK), BF16),
            pltpu.VMEM((NY, 2, BLOCK), F32),
            pltpu.VMEM((15, 2, BLOCK), F32),
            pltpu.VMEM((4, BLOCK), F32),
            pltpu.VMEM((11, 4, BLOCK), F32),
            pltpu.VMEM((NY, NX, BLOCK), F32),
            dma((4,)), dma((4,)), dma((3,)), dma((3,)), dma((4,)), dma((4,)),
            dma((ITERS, 7)), dma((ITERS, 7)), dma((early, 7)), dma((early, 7)),
            dma((early, 11)), dma((early, 11)), dma((15,)), dma((15,)), dma((11,)), dma((11,)),
            dma((3,)), dma((3,)), dma((3, 2)), dma((3, 2)), dma((3, 2)), dma((3, 2)), dma((3,)), dma((3,)),
            dma((2,)), pltpu.SemaphoreType.REGULAR, pltpu.SemaphoreType.REGULAR,
        ],
        compiler_params=pltpu.CompilerParams(
            collective_id=0, has_side_effects=True, vmem_limit_bytes=24 << 20
        ),
    )(*(pltpu.with_memory_space_constraint(array, pltpu.HBM) for array in (features, prototypes)))
    return (scaled * rows.reshape(ROWS)[:, None]).astype(BF16)


def solution(mesh):
    in_specs = (P("batch", None), P(("proto", "batch"), None))
    out_specs = P("batch", "proto")
    return jax.shard_map(local, mesh=mesh, in_specs=in_specs, out_specs=out_specs, check_vma=False)
```

```python
import jax
import jax.numpy as jnp
from jax import lax
from jax.experimental import pallas as pl
from jax.experimental.pallas import tpu as pltpu
from jax.sharding import PartitionSpec as P

ITERS = 3
NX, NY, NZ, RING = 4, 4, 12, 8
ROWS, COLS, DEPTH, BLOCK = 512, 2048, 256, 128
TILE, HALF = 1024, 256
PIECE = 64
TOTAL_PROTOS = 98304.0
MESH = pl.DeviceIdType.MESH
NT = (((1,), (1,)), ((), ()))
F32, BF16 = jnp.float32, jnp.bfloat16


def unit_rows(values):
    values = values.astype(F32)
    scale = lax.rsqrt(1e-06 + jnp.sum(values * values, axis=1, keepdims=True))
    return (values * scale).astype(BF16)


def split(values):
    high = values.astype(BF16)
    low = (values - high.astype(F32)).astype(BF16)
    return jnp.concatenate([high, low], axis=0)


def kernel(
    feat_ref, proto_ref, scaled_ref, row_ref,
    loaded, own_feat, feats, unit_feats, protos, other, unit_protos, weights, across,
    col_own, col_in, ring_own, ring_in, z_own, z_in, last_own, last_in, lastz_own, lastz_in, col_last,
    fs, fr, ps, pr, gs, gr, cs, cr, ys, yr, zs, zr, ls, lr, lzs, lzr, bs, br, es, er, hs, hr, ks, kr, ms, token_a, token_b,
):
    batch, proto = lax.axis_index("batch"), lax.axis_index("proto")
    x = lax.div(batch, NY)
    yl = batch - NY * x
    yh = lax.div(proto + 8, 32)
    pair = lax.div(proto, 2)
    z, core = pair - NZ * yh, proto - 2 * pair
    y = yh * NY + yl
    mate = 1 - core

    def device(px, py, pz, pcore):
        high = lax.div(py, NY)
        return {"batch": (px - high) * NY + py, "proto": (high * NZ + pz) * 2 + pcore}

    xs = [x] + [x + d - NX * lax.div(x + d, NX) for d in range(1, NX)]
    ry = [y] + [y + d - RING * lax.div(y + d, RING) for d in range(1, RING)]
    rz = [z] + [z + d - NZ * lax.div(z + d + 4, 16) for d in range(1, NZ)]
    near_y = [yl, yl + 1 - 2 * (yl - 2 * lax.div(yl, 2)), yl + 2 - NY * lax.div(yl, 2), NY - 1 - yl]
    col_peers = [device(xs[d], y, z, c) for d in (2, 1, 3) for c in (core, mate)]
    col_peers.append(device(x, y, z, mate))
    far_y = [ry[d] for d in (4, 3, 5, 2, 6, 1, 7)]
    ring_peers = [device(x, py, z, core) for py in far_y]
    last_peers = [(py, device(x, py, z, core)) for py in far_y]
    last_peers += [(py, device(x, py, z, mate)) for py in far_y + [y]]
    z_peers = [device(x, y, rz[d], core) for d in (6, 5, 7, 4, 8, 3, 9, 2, 10, 1, 11)]

    def signal(semaphore, peers):
        for peer in peers:
            pl.semaphore_signal(semaphore, inc=1, device_id=peer, device_id_type=MESH)

    two_y = [device(x, py, z, core) for py in (ry[2], ry[6])]
    one_y = [device(x, py, z, core) for py in (ry[1], ry[7])]
    two_z = [device(x, y, pz, core) for pz in (rz[2], rz[10])]
    one_z = [device(x, y, pz, core) for pz in (rz[1], rz[11])]
    barrier = pltpu.get_barrier_semaphore()
    partners = two_y + two_z + col_peers + one_y + one_z
    signal(barrier, partners)
    loads = [
        pltpu.make_async_copy(feat_ref, loaded, ms.at[0]),
        pltpu.make_async_copy(proto_ref, protos.at[batch], ms.at[1]),
    ]
    for load in loads:
        load.start()
    pl.semaphore_wait(barrier, len(partners))

    sent = []

    def remote(src, dst, send, recv, peer):
        copy = pltpu.make_async_remote_copy(
            src_ref=src, dst_ref=dst, send_sem=send, recv_sem=recv,
            device_id=peer, device_id_type=MESH,
        )
        copy.start()
        sent.append(copy)
        return copy

    proto_copies = [
        remote(proto_ref, protos.at[batch], ps.at[d - 1], pr.at[d - 1], device(xs[d], y, z, core))
        for d in (2, 1, 3)
    ]
    mine = pl.ds(pl.multiple_of(core * HALF, HALF), HALF)
    feat_copies = []
    for i, peer in ((0, two_y[0]), (1, two_y[1]), (0, one_y[0]), (0, one_y[1]), (1, one_y[0]), (1, one_y[1])):
        src = feat_ref.at[pl.ds(pl.multiple_of(core * HALF + i * BLOCK, BLOCK), BLOCK)]
        slot = len(feat_copies)
        feat_copies.append(
            remote(src, feats.at[yl, pl.ds(i * BLOCK, BLOCK)], fs.at[slot], fr.at[slot], peer)
        )
    partner = device(x, y, z, mate)
    mate_copies = [remote(proto_ref, other.at[x], gs.at[0], gr.at[0], partner)]
    signal(token_a, two_y + two_z + one_y)

    def place(ref, block, values):
        ref[pl.ds(pl.multiple_of(block * BLOCK, BLOCK), values.shape[0]), :] = values

    def fill(block, count):
        rows = pl.ds(pl.multiple_of(block * BLOCK, BLOCK), count)
        for k in range(0, TILE, HALF):
            scores = lax.dot_general(
                unit_feats[rows, :], unit_protos[k:k + HALF, :], NT, preferred_element_type=F32
            )
            weights[rows, k:k + HALF] = jnp.exp(20.0 * scores).astype(BF16)

    loads[0].wait()
    own_feat[...] = unit_rows(loaded[...])
    place(unit_feats, yl * 2, own_feat[mine, :])
    loads[1].wait()
    place(unit_protos, core * NX + x, unit_rows(protos[batch]))
    for slot, d in ((1, 3), (2, 1), (0, 2)):
        proto_copies[slot].wait_recv()
        arrived = protos.at[xs[d] * NY + yl]
        mate_copies.append(
            remote(arrived, other.at[xs[d]], gs.at[len(mate_copies)], gr.at[len(mate_copies)], partner)
        )
        place(unit_protos, core * NX + xs[d], unit_rows(arrived[...]))
    pl.semaphore_wait(token_a, 6)
    signal(token_b, two_y + two_z)
    for copy, px in zip(mate_copies, (x, xs[3], xs[1], xs[2])):
        copy.wait_recv()
        place(unit_protos, mate * NX + px, unit_rows(other[px]))
    fill(yl * 2, HALF)
    for slot, shift, i in ((0, 2, 0), (1, 2, 1), (2, 3, 0), (3, 1, 0), (4, 3, 1), (5, 1, 1)):
        feat_copies[slot].wait_recv()
        source = yl + shift - NY * lax.div(yl + shift, NY)
        place(unit_feats, source * 2 + i, unit_rows(feats[source, i * BLOCK:(i + 1) * BLOCK]))
        fill(source * 2 + i, BLOCK)

    tile_mask = lax.broadcasted_iota(jnp.int32, (8, TILE), 1) // BLOCK == lax.broadcasted_iota(
        jnp.int32, (8, TILE), 0
    )
    row_of = lax.broadcasted_iota(jnp.int32, (8, BLOCK), 0)

    def fold(wide):
        part = wide[:, :BLOCK]
        for k in range(1, 8):
            part = jnp.where(row_of == k, wide[:, k * BLOCK:(k + 1) * BLOCK], part)
        return part

    def column_sums(factor):
        wide = jnp.concatenate(
            [jnp.broadcast_to(factor[k:k + 1], (8, BLOCK)) for k in range(8)], axis=1
        )
        summed = jnp.dot(split(wide), weights[...], preferred_element_type=F32)
        return fold(summed[:8] + summed[8:])

    def row_sums(factor):
        wide = jnp.where(tile_mask, jnp.concatenate([factor] * 8, axis=1), 0.0)
        summed = jnp.dot(split(wide), across[...], preferred_element_type=F32)
        return fold(jnp.broadcast_to(jnp.sum(summed, axis=0, keepdims=True), (8, TILE)))

    def start(value, own, slots, send, recv, peers):
        own[...] = value.astype(own.dtype)
        return [remote(own, slots.at[i], send.at[i], recv.at[i], peer) for i, peer in enumerate(peers)]

    def finish(total, slots, copies):
        for i, copy in enumerate(copies):
            copy.wait_recv()
            total = total + slots[i].astype(F32)
        return total

    half = BLOCK // 2
    row_factor = jnp.ones((8, BLOCK), F32)
    for step in range(ITERS):
        part = column_sums(row_factor)
        copies = start(part, col_own.at[step], col_in.at[step], cs.at[step], cr.at[step], col_peers)
        if step == 0:
            for k in range(0, TILE, HALF):
                for j in range(0, TILE, HALF):
                    scores = lax.dot_general(
                        unit_protos[k:k + HALF, :], unit_feats[j:j + HALF, :], NT,
                        preferred_element_type=F32,
                    )
                    across[k:k + HALF, j:j + HALF] = jnp.exp(20.0 * scores).astype(BF16)
            pl.semaphore_wait(token_b, 4)
        part = finish(part, col_in.at[step], copies)
        col_factor = 1.0 / part
        if step == 1:
            for copy in y_copies:
                copy.wait_recv()
            x_copies = []
            for k in range(1, NY):
                block = protos.at[x * NY + near_y[k]]
                for side, d in enumerate((1, 3)):
                    x_copies.append(
                        remote(block, block, es.at[k - 1, side], er.at[k - 1, side], device(xs[d], y, z, core))
                    )
        part = row_sums(col_factor)
        if step == ITERS - 1:
            last_col = jnp.where(core == 0, col_factor[:4], col_factor[4:]) * TOTAL_PROTOS
            col_last[yl] = last_col
            for k in range(4):
                last_own[k] = part[2 * k:2 * k + 2].astype(BF16)
            copies = [
                remote(last_own.at[py - NY * lax.div(py, NY)], last_in.at[i], ls.at[i], lr.at[i], peer)
                for i, (py, peer) in enumerate(last_peers)
            ]
            k_copies = [
                remote(col_last.at[yl], col_last.at[yl], ks.at[k - 1], kr.at[k - 1],
                       device(x, yh * NY + near_y[k], z, core))
                for k in range(1, NY)
            ]
            mine_sum = last_own[yl].astype(F32)
            mate_sum = jnp.zeros((2, BLOCK), F32)
            for i, copy in enumerate(copies):
                copy.wait_recv()
                if i < 7:
                    mine_sum = mine_sum + last_in[i].astype(F32)
                else:
                    mate_sum = mate_sum + last_in[i].astype(F32)
            first = jnp.where(core == 0, mine_sum, mate_sum)
            second = jnp.where(core == 0, mate_sum, mine_sum)
            part = jnp.concatenate([first, second], axis=0)
            copies = start(part, lastz_own, lastz_in, lzs, lzr, z_peers)
            for copy in f_copies:
                copy.wait_recv()
            for copy in k_copies:
                copy.wait_recv()
            for b in range(NX * NY):
                scores = lax.dot_general(
                    own_feat[...], unit_rows(protos[b]), NT, preferred_element_type=F32
                )
                factor = col_last[b % NY, b // NY:b // NY + 1, :]
                scaled_ref[:, b * BLOCK:(b + 1) * BLOCK] = jnp.exp(20.0 * scores) * factor
            for copy in sent[:-len(copies)]:
                copy.wait_send()
            row_ref[...] = 1.0 / finish(part, lastz_in, copies)
            for copy in copies:
                copy.wait_send()
            break
        copies = start(part, ring_own.at[step], ring_in.at[step], ys.at[step], yr.at[step], ring_peers)
        part = finish(part, ring_in.at[step], copies)
        copies = start(part, z_own.at[step], z_in.at[step], zs.at[step], zr.at[step], z_peers)
        if step == 0:
            block = protos.at[batch]
            y_copies = [
                remote(block, block, bs.at[k - 1], br.at[k - 1], device(x, yh * NY + near_y[k], z, core))
                for k in range(1, NY)
            ]
        else:
            f_copies = []
            for k in range(1, NY):
                for side, (source, d) in enumerate(((xs[3], 1), (xs[1], 3))):
                    x_copies[2 * (k - 1) + side].wait_recv()
                    piece = protos.at[source * NY + near_y[k], pl.ds(side * half, half)]
                    f_copies.append(
                        remote(piece, piece, hs.at[k - 1, side], hr.at[k - 1, side], device(xs[d], y, z, core))
                    )
        row_factor = 1.0 / finish(part, z_in.at[step], copies)


def scale_rows(scaled_ref, row_ref, out_ref, rounded, sems):
    copies = []
    for k in range(ROWS // BLOCK):
        column = jnp.broadcast_to(row_ref[k:k + 1, :], (BLOCK, BLOCK)).T
        for first in range(0, BLOCK, PIECE):
            rows = pl.ds(k * BLOCK + first, PIECE)
            factor = jnp.concatenate([column[first:first + PIECE]] * (COLS // BLOCK), axis=1)
            rounded[rows, :] = (scaled_ref[rows, :] * factor).astype(BF16)
            copies.append(
                pltpu.make_async_copy(rounded.at[rows], out_ref.at[rows], sems.at[len(copies)])
            )
            copies[-1].start()
    for copy in copies:
        copy.wait()


def local(features, prototypes):
    vmem = pl.BlockSpec(memory_space=pltpu.VMEM)
    hbm = pl.BlockSpec(memory_space=pltpu.HBM)
    dma = pltpu.SemaphoreType.DMA
    early = ITERS - 1
    scaled, rows = pl.pallas_call(
        kernel,
        out_shape=(
            jax.ShapeDtypeStruct((ROWS, COLS), F32),
            jax.ShapeDtypeStruct((4, BLOCK), F32),
        ),
        in_specs=[hbm, hbm],
        out_specs=(vmem, vmem),
        scratch_shapes=[
            pltpu.VMEM((ROWS, DEPTH), BF16),
            pltpu.VMEM((ROWS, DEPTH), BF16),
            pltpu.VMEM((NY, HALF, DEPTH), BF16),
            pltpu.VMEM((TILE, DEPTH), BF16),
            pltpu.VMEM((NX * NY, BLOCK, DEPTH), BF16),
            pltpu.VMEM((NX, BLOCK, DEPTH), BF16),
            pltpu.VMEM((TILE, DEPTH), BF16),
            pltpu.VMEM((TILE, TILE), BF16),
            pltpu.VMEM((TILE, TILE), BF16),
            pltpu.VMEM((ITERS, 8, BLOCK), BF16),
            pltpu.VMEM((ITERS, 7, 8, BLOCK), BF16),
            pltpu.VMEM((early, 8, BLOCK), BF16),
            pltpu.VMEM((early, 7, 8, BLOCK), BF16),
            pltpu.VMEM((early, 8, BLOCK), BF16),
            pltpu.VMEM((early, 11, 8, BLOCK), BF16),
            pltpu.VMEM((NY, 2, BLOCK), BF16),
            pltpu.VMEM((15, 2, BLOCK), BF16),
            pltpu.VMEM((4, BLOCK), BF16),
            pltpu.VMEM((11, 4, BLOCK), BF16),
            pltpu.VMEM((NY, NX, BLOCK), F32),
            dma((6,)), dma((6,)), dma((3,)), dma((3,)), dma((4,)), dma((4,)),
            dma((ITERS, 7)), dma((ITERS, 7)), dma((early, 7)), dma((early, 7)),
            dma((early, 11)), dma((early, 11)), dma((15,)), dma((15,)), dma((11,)), dma((11,)),
            dma((3,)), dma((3,)), dma((3, 2)), dma((3, 2)), dma((3, 2)), dma((3, 2)), dma((3,)), dma((3,)),
            dma((2,)), pltpu.SemaphoreType.REGULAR, pltpu.SemaphoreType.REGULAR,
        ],
        compiler_params=pltpu.CompilerParams(
            collective_id=0, has_side_effects=True, vmem_limit_bytes=24 << 20
        ),
    )(*(pltpu.with_memory_space_constraint(array, pltpu.HBM) for array in (features, prototypes)))
    pieces = ROWS // PIECE
    return pl.pallas_call(
        scale_rows,
        out_shape=jax.ShapeDtypeStruct((ROWS, COLS), BF16),
        in_specs=[vmem, vmem],
        out_specs=pl.BlockSpec(memory_space=pltpu.HBM),
        scratch_shapes=[pltpu.VMEM((ROWS, COLS), BF16), dma((pieces,))],
        compiler_params=pltpu.CompilerParams(vmem_limit_bytes=16 << 20),
    )(scaled, rows)


def solution(mesh):
    in_specs = (P("batch", None), P(("proto", "batch"), None))
    out_specs = P("batch", "proto")
    return jax.shard_map(local, mesh=mesh, in_specs=in_specs, out_specs=out_specs, check_vma=False)
```

```python
import jax
import jax.numpy as jnp
from jax import lax
from jax.experimental import pallas as pl
from jax.experimental.pallas import tpu as pltpu
from jax.sharding import PartitionSpec as P

ITERS = 3
NX, NY, NZ, RING = 4, 4, 12, 8
ROWS, COLS, DEPTH, BLOCK = 512, 2048, 256, 128
TILE, HALF = 1024, 256
PIECE = 64
TOTAL_PROTOS = 98304.0
MESH = pl.DeviceIdType.MESH
NT = (((1,), (1,)), ((), ()))
F32, BF16 = jnp.float32, jnp.bfloat16


def unit_rows(values):
    values = values.astype(F32)
    scale = lax.rsqrt(1e-06 + jnp.sum(values * values, axis=1, keepdims=True))
    return (values * scale).astype(BF16)


def split(values):
    high = values.astype(BF16)
    low = (values - high.astype(F32)).astype(BF16)
    return jnp.concatenate([high, low], axis=0)


def kernel(
    feat_ref, proto_ref, scaled_ref, row_ref,
    loaded, own_feat, feats, unit_feats, protos, other, unit_protos, weights, across,
    col_own, col_in, ring_own, ring_in, z_own, z_in, last_own, last_in, lastz_own, lastz_in, col_last,
    fs, fr, ps, pr, gs, gr, cs, cr, ys, yr, zs, zr, ls, lr, lzs, lzr, bs, br, es, er, hs, hr, ks, kr, ms, token_a, token_b, totals,
    far_in, ds, dr,
):
    batch, proto = lax.axis_index("batch"), lax.axis_index("proto")
    x = lax.div(batch, NY)
    yl = batch - NY * x
    yh = lax.div(proto + 8, 32)
    pair = lax.div(proto, 2)
    z, core = pair - NZ * yh, proto - 2 * pair
    y = yh * NY + yl
    mate = 1 - core

    def device(px, py, pz, pcore):
        high = lax.div(py, NY)
        return {"batch": (px - high) * NY + py, "proto": (high * NZ + pz) * 2 + pcore}

    xs = [x] + [x + d - NX * lax.div(x + d, NX) for d in range(1, NX)]
    ry = [y] + [y + d - RING * lax.div(y + d, RING) for d in range(1, RING)]
    rz = [z] + [z + d - NZ * lax.div(z + d + 4, 16) for d in range(1, NZ)]
    near_y = [yl, yl + 1 - 2 * (yl - 2 * lax.div(yl, 2)), yl + 2 - NY * lax.div(yl, 2), NY - 1 - yl]
    col_peers = [device(xs[d], y, z, c) for d in (2, 1, 3) for c in (core, mate)]
    col_peers.append(device(x, y, z, mate))
    far_y = [ry[d] for d in (4, 3, 5, 2, 6, 1, 7)]
    ring_peers = [device(x, py, z, core) for py in far_y]
    last_peers = [(py, device(x, py, z, core)) for py in far_y]
    last_peers += [(py, device(x, py, z, mate)) for py in far_y + [y]]
    z_peers = [device(x, y, rz[d], core) for d in (6, 5, 7, 4, 8, 3, 9, 2, 10, 1, 11)]
    far_peers = [device(x, py, rz[6], core) for py in far_y + [y]]

    def signal(semaphore, peers):
        for peer in peers:
            pl.semaphore_signal(semaphore, inc=1, device_id=peer, device_id_type=MESH)

    two_y = [device(x, py, z, core) for py in (ry[2], ry[6])]
    one_y = [device(x, py, z, core) for py in (ry[1], ry[7])]
    two_z = [device(x, y, pz, core) for pz in (rz[2], rz[10])]
    one_z = [device(x, y, pz, core) for pz in (rz[1], rz[11])]
    barrier = pltpu.get_barrier_semaphore()
    partners = two_y + two_z + col_peers + one_y + one_z
    signal(barrier, partners)
    loads = [
        pltpu.make_async_copy(feat_ref, loaded, ms.at[0]),
        pltpu.make_async_copy(proto_ref, protos.at[batch], ms.at[1]),
    ]
    for load in loads:
        load.start()
    pl.semaphore_wait(barrier, len(partners))

    sent = []

    def remote(src, dst, send, recv, peer):
        copy = pltpu.make_async_remote_copy(
            src_ref=src, dst_ref=dst, send_sem=send, recv_sem=recv,
            device_id=peer, device_id_type=MESH,
        )
        copy.start()
        sent.append(copy)
        return copy

    proto_copies = [
        remote(proto_ref, protos.at[batch], ps.at[d - 1], pr.at[d - 1], device(xs[d], y, z, core))
        for d in (2, 1, 3)
    ]
    mine = pl.ds(pl.multiple_of(core * HALF, HALF), HALF)
    feat_copies = []
    for i, peer in ((0, two_y[0]), (1, two_y[1]), (0, one_y[0]), (0, one_y[1]), (1, one_y[0]), (1, one_y[1])):
        src = feat_ref.at[pl.ds(pl.multiple_of(core * HALF + i * BLOCK, BLOCK), BLOCK)]
        slot = len(feat_copies)
        feat_copies.append(
            remote(src, feats.at[yl, pl.ds(i * BLOCK, BLOCK)], fs.at[slot], fr.at[slot], peer)
        )
    partner = device(x, y, z, mate)
    mate_copies = [remote(proto_ref, other.at[x], gs.at[0], gr.at[0], partner)]
    signal(token_a, two_y + two_z + one_y)

    def place(ref, block, values):
        ref[pl.ds(pl.multiple_of(block * BLOCK, BLOCK), values.shape[0]), :] = values

    totals[...] = jnp.zeros_like(totals)
    ours, theirs = (core * NX, core * NX + 2), (mate * NX, mate * NX + 2)

    def fill(block, count, pairs):
        rows = pl.ds(pl.multiple_of(block * BLOCK, BLOCK), count)
        for pair in pairs:
            columns = pl.ds(pl.multiple_of(pair * BLOCK, HALF), HALF)
            scores = lax.dot_general(
                unit_feats[rows, :], unit_protos[columns, :], NT, preferred_element_type=F32
            )
            values = jnp.exp(20.0 * scores)
            weights[rows, columns] = values.astype(BF16)
            totals[:, columns] += jnp.sum(values.reshape(count // 8, 8, HALF), axis=0)

    loads[0].wait()
    own_feat[...] = unit_rows(loaded[...])
    place(unit_feats, yl * 2, own_feat[mine, :])
    loads[1].wait()
    place(unit_protos, core * NX + x, unit_rows(protos[batch]))
    for slot, d in ((1, 3), (2, 1), (0, 2)):
        proto_copies[slot].wait_recv()
        arrived = protos.at[xs[d] * NY + yl]
        mate_copies.append(
            remote(arrived, other.at[xs[d]], gs.at[len(mate_copies)], gr.at[len(mate_copies)], partner)
        )
        place(unit_protos, core * NX + xs[d], unit_rows(arrived[...]))
    pl.semaphore_wait(token_a, 6)
    signal(token_b, two_y + two_z)
    def take(slot, source, i):
        feat_copies[slot].wait_recv()
        place(unit_feats, source * 2 + i, unit_rows(feats[source, i * BLOCK:(i + 1) * BLOCK]))

    fill(yl * 2, HALF, ours)
    source = yl + 2 - NY * lax.div(yl + 2, NY)
    take(0, source, 0)
    take(1, source, 1)
    fill(source * 2, HALF, ours)
    for copy, px in zip(mate_copies, (x, xs[3], xs[1], xs[2])):
        copy.wait_recv()
        place(unit_protos, mate * NX + px, unit_rows(other[px]))
    fill(yl * 2, HALF, theirs)
    fill(source * 2, HALF, theirs)
    for slot, shift, i in ((2, 3, 0), (3, 1, 0), (4, 3, 1), (5, 1, 1)):
        source = yl + shift - NY * lax.div(yl + shift, NY)
        take(slot, source, i)
        fill(source * 2 + i, BLOCK, ours + theirs)

    tile_mask = lax.broadcasted_iota(jnp.int32, (8, TILE), 1) // BLOCK == lax.broadcasted_iota(
        jnp.int32, (8, TILE), 0
    )
    row_of = lax.broadcasted_iota(jnp.int32, (8, BLOCK), 0)

    def fold(wide):
        part = wide[:, :BLOCK]
        for k in range(1, 8):
            part = jnp.where(row_of == k, wide[:, k * BLOCK:(k + 1) * BLOCK], part)
        return part

    def column_sums(factor):
        wide = jnp.concatenate(
            [jnp.broadcast_to(factor[k:k + 1], (8, BLOCK)) for k in range(8)], axis=1
        )
        summed = jnp.dot(split(wide), weights[...], preferred_element_type=F32)
        return fold(summed[:8] + summed[8:])

    def row_sums(factor):
        wide = jnp.where(tile_mask, jnp.concatenate([factor] * 8, axis=1), 0.0)
        summed = jnp.dot(split(wide), across[...], preferred_element_type=F32)
        return fold(jnp.broadcast_to(jnp.sum(summed, axis=0, keepdims=True), (8, TILE)))

    def start(value, own, slots, send, recv, peers):
        own[...] = value.astype(own.dtype)
        return [remote(own, slots.at[i], send.at[i], recv.at[i], peer) for i, peer in enumerate(peers)]

    def finish(total, slots, copies):
        for i, copy in enumerate(copies):
            copy.wait_recv()
            total = total + slots[i].astype(F32)
        return total

    half = BLOCK // 2
    for step in range(ITERS):
        if step:
            part = column_sums(row_factor)
        else:
            summed = jnp.sum(totals[...], axis=0, keepdims=True)
            part = fold(jnp.broadcast_to(summed, (8, TILE)))
        copies = start(part, col_own.at[step], col_in.at[step], cs.at[step], cr.at[step], col_peers)
        if step == 0:
            for k in range(0, TILE, HALF):
                for j in range(0, TILE, HALF):
                    scores = lax.dot_general(
                        unit_protos[k:k + HALF, :], unit_feats[j:j + HALF, :], NT,
                        preferred_element_type=F32,
                    )
                    across[k:k + HALF, j:j + HALF] = jnp.exp(20.0 * scores).astype(BF16)
            pl.semaphore_wait(token_b, 4)
        part = finish(part, col_in.at[step], copies)
        col_factor = 1.0 / part
        if step == 1:
            for copy in y_copies:
                copy.wait_recv()
            x_copies = []
            for k in range(1, NY):
                block = protos.at[x * NY + near_y[k]]
                for side, d in enumerate((1, 3)):
                    x_copies.append(
                        remote(block, block, es.at[k - 1, side], er.at[k - 1, side], device(xs[d], y, z, core))
                    )
        part = row_sums(col_factor)
        if step == ITERS - 1:
            last_col = jnp.where(core == 0, col_factor[:4], col_factor[4:]) * TOTAL_PROTOS
            col_last[yl] = last_col
            for k in range(4):
                last_own[k] = part[2 * k:2 * k + 2].astype(BF16)
            copies = [
                remote(last_own.at[py - NY * lax.div(py, NY)], last_in.at[i], ls.at[i], lr.at[i], peer)
                for i, (py, peer) in enumerate(last_peers)
            ]
            k_copies = [
                remote(col_last.at[yl], col_last.at[yl], ks.at[k - 1], kr.at[k - 1],
                       device(x, yh * NY + near_y[k], z, core))
                for k in range(1, NY)
            ]
            mine_sum = last_own[yl].astype(F32)
            mate_sum = jnp.zeros((2, BLOCK), F32)
            for i, copy in enumerate(copies):
                copy.wait_recv()
                if i < 7:
                    mine_sum = mine_sum + last_in[i].astype(F32)
                else:
                    mate_sum = mate_sum + last_in[i].astype(F32)
            first = jnp.where(core == 0, mine_sum, mate_sum)
            second = jnp.where(core == 0, mate_sum, mine_sum)
            part = jnp.concatenate([first, second], axis=0)
            copies = start(part, lastz_own, lastz_in, lzs, lzr, z_peers)
            for copy in f_copies:
                copy.wait_recv()
            for copy in k_copies:
                copy.wait_recv()
            for b in range(NX * NY):
                scores = lax.dot_general(
                    own_feat[...], unit_rows(protos[b]), NT, preferred_element_type=F32
                )
                factor = col_last[b % NY, b // NY:b // NY + 1, :]
                scaled_ref[:, b * BLOCK:(b + 1) * BLOCK] = jnp.exp(20.0 * scores) * factor
            for copy in sent[:-len(copies)]:
                copy.wait_send()
            row_ref[...] = 1.0 / finish(part, lastz_in, copies)
            for copy in copies:
                copy.wait_send()
            break
        copies = start(part, ring_own.at[step], ring_in.at[step], ys.at[step], yr.at[step], ring_peers)
        far_copies = []
        if step:
            far_copies = [
                remote(ring_own.at[step], far_in.at[i], ds.at[i], dr.at[i], peer)
                for i, peer in enumerate(far_peers)
            ]
        part = finish(part, ring_in.at[step], copies)
        peers = z_peers[1:] if step else z_peers
        copies = start(part, z_own.at[step], z_in.at[step], zs.at[step], zr.at[step], peers)
        if step == 0:
            block = protos.at[batch]
            y_copies = [
                remote(block, block, bs.at[k - 1], br.at[k - 1], device(x, yh * NY + near_y[k], z, core))
                for k in range(1, NY)
            ]
        else:
            f_copies = []
            for k in range(1, NY):
                for side, (source, d) in enumerate(((xs[3], 1), (xs[1], 3))):
                    x_copies[2 * (k - 1) + side].wait_recv()
                    piece = protos.at[source * NY + near_y[k], pl.ds(side * half, half)]
                    f_copies.append(
                        remote(piece, piece, hs.at[k - 1, side], hr.at[k - 1, side], device(xs[d], y, z, core))
                    )
        part = finish(part, z_in.at[step], copies)
        row_factor = 1.0 / finish(part, far_in, far_copies)


def scale_rows(scaled_ref, row_ref, out_ref, rounded, sems):
    copies = []
    for k in range(ROWS // BLOCK):
        column = jnp.broadcast_to(row_ref[k:k + 1, :], (BLOCK, BLOCK)).T
        for first in range(0, BLOCK, PIECE):
            rows = pl.ds(k * BLOCK + first, PIECE)
            factor = jnp.concatenate([column[first:first + PIECE]] * (COLS // BLOCK), axis=1)
            rounded[rows, :] = (scaled_ref[rows, :] * factor).astype(BF16)
            copies.append(
                pltpu.make_async_copy(rounded.at[rows], out_ref.at[rows], sems.at[len(copies)])
            )
            copies[-1].start()
    for copy in copies:
        copy.wait()


def local(features, prototypes):
    vmem = pl.BlockSpec(memory_space=pltpu.VMEM)
    hbm = pl.BlockSpec(memory_space=pltpu.HBM)
    dma = pltpu.SemaphoreType.DMA
    early = ITERS - 1
    scaled, rows = pl.pallas_call(
        kernel,
        out_shape=(
            jax.ShapeDtypeStruct((ROWS, COLS), F32),
            jax.ShapeDtypeStruct((4, BLOCK), F32),
        ),
        in_specs=[hbm, hbm],
        out_specs=(vmem, vmem),
        scratch_shapes=[
            pltpu.VMEM((ROWS, DEPTH), BF16),
            pltpu.VMEM((ROWS, DEPTH), BF16),
            pltpu.VMEM((NY, HALF, DEPTH), BF16),
            pltpu.VMEM((TILE, DEPTH), BF16),
            pltpu.VMEM((NX * NY, BLOCK, DEPTH), BF16),
            pltpu.VMEM((NX, BLOCK, DEPTH), BF16),
            pltpu.VMEM((TILE, DEPTH), BF16),
            pltpu.VMEM((TILE, TILE), BF16),
            pltpu.VMEM((TILE, TILE), BF16),
            pltpu.VMEM((ITERS, 8, BLOCK), BF16),
            pltpu.VMEM((ITERS, 7, 8, BLOCK), BF16),
            pltpu.VMEM((early, 8, BLOCK), BF16),
            pltpu.VMEM((early, 7, 8, BLOCK), BF16),
            pltpu.VMEM((early, 8, BLOCK), BF16),
            pltpu.VMEM((early, 11, 8, BLOCK), BF16),
            pltpu.VMEM((NY, 2, BLOCK), BF16),
            pltpu.VMEM((15, 2, BLOCK), BF16),
            pltpu.VMEM((4, BLOCK), BF16),
            pltpu.VMEM((11, 4, BLOCK), BF16),
            pltpu.VMEM((NY, NX, BLOCK), F32),
            dma((6,)), dma((6,)), dma((3,)), dma((3,)), dma((4,)), dma((4,)),
            dma((ITERS, 7)), dma((ITERS, 7)), dma((early, 7)), dma((early, 7)),
            dma((early, 11)), dma((early, 11)), dma((15,)), dma((15,)), dma((11,)), dma((11,)),
            dma((3,)), dma((3,)), dma((3, 2)), dma((3, 2)), dma((3, 2)), dma((3, 2)), dma((3,)), dma((3,)),
            dma((2,)), pltpu.SemaphoreType.REGULAR, pltpu.SemaphoreType.REGULAR,
            pltpu.VMEM((8, TILE), F32),
            pltpu.VMEM((8, 8, BLOCK), BF16), dma((8,)), dma((8,)),
        ],
        compiler_params=pltpu.CompilerParams(
            collective_id=0, has_side_effects=True, vmem_limit_bytes=24 << 20
        ),
    )(*(pltpu.with_memory_space_constraint(array, pltpu.HBM) for array in (features, prototypes)))
    pieces = ROWS // PIECE
    return pl.pallas_call(
        scale_rows,
        out_shape=jax.ShapeDtypeStruct((ROWS, COLS), BF16),
        in_specs=[vmem, vmem],
        out_specs=pl.BlockSpec(memory_space=pltpu.HBM),
        scratch_shapes=[pltpu.VMEM((ROWS, COLS), BF16), dma((pieces,))],
        compiler_params=pltpu.CompilerParams(vmem_limit_bytes=16 << 20),
    )(scaled, rows)


def solution(mesh):
    in_specs = (P("batch", None), P(("proto", "batch"), None))
    out_specs = P("batch", "proto")
    return jax.shard_map(local, mesh=mesh, in_specs=in_specs, out_specs=out_specs, check_vma=False)
```

```python
import jax
import jax.numpy as jnp
from jax import lax
from jax.experimental import pallas as pl
from jax.experimental.pallas import tpu as pltpu
from jax.sharding import PartitionSpec as P

ITERS = 3
NX, NY, NZ, RING = 4, 4, 12, 8
ROWS, COLS, DEPTH, BLOCK = 512, 2048, 256, 128
TILE, HALF = 1024, 256
PIECE = 64
TOTAL_PROTOS = 98304.0
MESH = pl.DeviceIdType.MESH
NT = (((1,), (1,)), ((), ()))
F32, BF16 = jnp.float32, jnp.bfloat16


def unit_rows(values):
    values = values.astype(F32)
    scale = lax.rsqrt(1e-06 + jnp.sum(values * values, axis=1, keepdims=True))
    return (values * scale).astype(BF16)


def split(values):
    high = values.astype(BF16)
    low = (values - high.astype(F32)).astype(BF16)
    return jnp.concatenate([high, low], axis=0)


def kernel(
    feat_ref, proto_ref, scaled_ref, row_ref,
    loaded, own_feat, feats, unit_feats, protos, other, unit_protos, weights, across,
    col_own, col_in, ring_own, ring_in, z_own, z_in, last_own, last_in, lastz_own, lastz_in, col_last,
    fs, fr, ps, pr, gs, gr, cs, cr, ys, yr, zs, zr, ls, lr, lzs, lzr, bs, br, es, er, hs, hr, ks, kr, ms, token_a, token_b, totals,
    far_in, ds, dr,
):
    batch, proto = lax.axis_index("batch"), lax.axis_index("proto")
    x = lax.div(batch, NY)
    yl = batch - NY * x
    yh = lax.div(proto + 8, 32)
    pair = lax.div(proto, 2)
    z, core = pair - NZ * yh, proto - 2 * pair
    y = yh * NY + yl
    mate = 1 - core

    def device(px, py, pz, pcore):
        high = lax.div(py, NY)
        return {"batch": (px - high) * NY + py, "proto": (high * NZ + pz) * 2 + pcore}

    xs = [x] + [x + d - NX * lax.div(x + d, NX) for d in range(1, NX)]

    def ring_at(d):
        return y + d - RING * lax.div(y + d, RING)

    def z_at(d):
        return z + d - NZ * lax.div(z + d + 4, 16)

    col_peers = [device(xs[d], y, z, c) for d in (2, 1, 3) for c in (core, mate)]
    col_peers.append(device(x, y, z, mate))
    def signal(semaphore, peers):
        for peer in peers:
            pl.semaphore_signal(semaphore, inc=1, device_id=peer, device_id_type=MESH)

    two_y = [device(x, py, z, core) for py in (ring_at(2), ring_at(6))]
    one_y = [device(x, py, z, core) for py in (ring_at(1), ring_at(7))]
    two_z = [device(x, y, pz, core) for pz in (z_at(2), z_at(10))]
    one_z = [device(x, y, pz, core) for pz in (z_at(1), z_at(11))]
    barrier = pltpu.get_barrier_semaphore()
    partners = two_y + two_z + col_peers + one_y + one_z
    signal(barrier, partners)
    loads = [
        pltpu.make_async_copy(feat_ref, loaded, ms.at[0]),
        pltpu.make_async_copy(proto_ref, protos.at[batch], ms.at[1]),
    ]
    for load in loads:
        load.start()
    pl.semaphore_wait(barrier, len(partners))

    sent = []

    def remote(src, dst, send, recv, peer):
        copy = pltpu.make_async_remote_copy(
            src_ref=src, dst_ref=dst, send_sem=send, recv_sem=recv,
            device_id=peer, device_id_type=MESH,
        )
        copy.start()
        sent.append(copy)
        return copy

    proto_copies = [
        remote(proto_ref, protos.at[batch], ps.at[d - 1], pr.at[d - 1], device(xs[d], y, z, core))
        for d in (2, 1, 3)
    ]
    mine = pl.ds(pl.multiple_of(core * HALF, HALF), HALF)
    feat_copies = []
    for i, peer in ((0, two_y[0]), (1, two_y[1]), (0, one_y[0]), (0, one_y[1]), (1, one_y[0]), (1, one_y[1])):
        src = feat_ref.at[pl.ds(pl.multiple_of(core * HALF + i * BLOCK, BLOCK), BLOCK)]
        slot = len(feat_copies)
        feat_copies.append(
            remote(src, feats.at[yl, pl.ds(i * BLOCK, BLOCK)], fs.at[slot], fr.at[slot], peer)
        )
    partner = device(x, y, z, mate)
    mate_copies = [remote(proto_ref, other.at[x], gs.at[0], gr.at[0], partner)]
    signal(token_a, two_y + two_z + one_y)

    near_y = [yl, yl + 1 - 2 * (yl - 2 * lax.div(yl, 2)), yl + 2 - NY * lax.div(yl, 2), NY - 1 - yl]
    far_y = [ring_at(d) for d in (4, 3, 5, 2, 6, 1, 7)]
    ring_peers = [device(x, py, z, core) for py in far_y]
    last_peers = [(py, device(x, py, z, core)) for py in far_y]
    last_peers += [(py, device(x, py, z, mate)) for py in far_y + [y]]
    z_peers = [device(x, y, z_at(d), core) for d in (6, 5, 7, 4, 8, 3, 9, 2, 10, 1, 11)]
    far_peers = [device(x, py, z_at(6), core) for py in far_y + [y]]

    def place(ref, block, values):
        ref[pl.ds(pl.multiple_of(block * BLOCK, BLOCK), values.shape[0]), :] = values

    totals[...] = jnp.zeros_like(totals)
    ours, theirs = (core * NX, core * NX + 2), (mate * NX, mate * NX + 2)

    def fill(block, count, pairs):
        rows = pl.ds(pl.multiple_of(block * BLOCK, BLOCK), count)
        for pair in pairs:
            columns = pl.ds(pl.multiple_of(pair * BLOCK, HALF), HALF)
            scores = lax.dot_general(
                unit_feats[rows, :], unit_protos[columns, :], NT, preferred_element_type=F32
            )
            values = jnp.exp(20.0 * scores)
            weights[rows, columns] = values.astype(BF16)
            totals[:, columns] += jnp.sum(values.reshape(count // 8, 8, HALF), axis=0)

    loads[0].wait()
    own_feat[...] = unit_rows(loaded[...])
    place(unit_feats, yl * 2, own_feat[mine, :])
    loads[1].wait()
    place(unit_protos, core * NX + x, unit_rows(protos[batch]))
    for slot, d in ((1, 3), (2, 1), (0, 2)):
        proto_copies[slot].wait_recv()
        arrived = protos.at[xs[d] * NY + yl]
        mate_copies.append(
            remote(arrived, other.at[xs[d]], gs.at[len(mate_copies)], gr.at[len(mate_copies)], partner)
        )
        place(unit_protos, core * NX + xs[d], unit_rows(arrived[...]))
    pl.semaphore_wait(token_a, 6)
    signal(token_b, two_y + two_z)
    def take(slot, source, i):
        feat_copies[slot].wait_recv()
        place(unit_feats, source * 2 + i, unit_rows(feats[source, i * BLOCK:(i + 1) * BLOCK]))

    fill(yl * 2, HALF, ours)
    source = yl + 2 - NY * lax.div(yl + 2, NY)
    take(0, source, 0)
    take(1, source, 1)
    fill(source * 2, HALF, ours)
    for copy, px in zip(mate_copies, (x, xs[3], xs[1], xs[2])):
        copy.wait_recv()
        place(unit_protos, mate * NX + px, unit_rows(other[px]))
    fill(yl * 2, HALF, theirs)
    fill(source * 2, HALF, theirs)
    for slot, shift, i in ((2, 3, 0), (3, 1, 0), (4, 3, 1), (5, 1, 1)):
        source = yl + shift - NY * lax.div(yl + shift, NY)
        take(slot, source, i)
        fill(source * 2 + i, BLOCK, ours + theirs)

    tile_mask = lax.broadcasted_iota(jnp.int32, (8, TILE), 1) // BLOCK == lax.broadcasted_iota(
        jnp.int32, (8, TILE), 0
    )
    row_of = lax.broadcasted_iota(jnp.int32, (8, BLOCK), 0)

    def fold(wide):
        part = wide[:, :BLOCK]
        for k in range(1, 8):
            part = jnp.where(row_of == k, wide[:, k * BLOCK:(k + 1) * BLOCK], part)
        return part

    def column_sums(factor):
        wide = jnp.concatenate(
            [jnp.broadcast_to(factor[k:k + 1], (8, BLOCK)) for k in range(8)], axis=1
        )
        summed = jnp.dot(split(wide), weights[...], preferred_element_type=F32)
        return fold(summed[:8] + summed[8:])

    def row_sums(factor):
        wide = jnp.where(tile_mask, jnp.concatenate([factor] * 8, axis=1), 0.0)
        summed = jnp.dot(split(wide), across[...], preferred_element_type=F32)
        return fold(jnp.broadcast_to(jnp.sum(summed, axis=0, keepdims=True), (8, TILE)))

    def start(value, own, slots, send, recv, peers):
        own[...] = value.astype(own.dtype)
        return [remote(own, slots.at[i], send.at[i], recv.at[i], peer) for i, peer in enumerate(peers)]

    def finish(total, slots, copies):
        for i, copy in enumerate(copies):
            copy.wait_recv()
            total = total + slots[i].astype(F32)
        return total

    half = BLOCK // 2
    for step in range(ITERS):
        if step:
            part = column_sums(row_factor)
        else:
            summed = jnp.sum(totals[...], axis=0, keepdims=True)
            part = fold(jnp.broadcast_to(summed, (8, TILE)))
        copies = start(part, col_own.at[step], col_in.at[step], cs.at[step], cr.at[step], col_peers)
        if step == 0:
            for k in range(0, TILE, HALF):
                for j in range(0, TILE, HALF):
                    scores = lax.dot_general(
                        unit_protos[k:k + HALF, :], unit_feats[j:j + HALF, :], NT,
                        preferred_element_type=F32,
                    )
                    across[k:k + HALF, j:j + HALF] = jnp.exp(20.0 * scores).astype(BF16)
            pl.semaphore_wait(token_b, 4)
        part = finish(part, col_in.at[step], copies)
        col_factor = 1.0 / part
        if step == 1:
            for copy in y_copies:
                copy.wait_recv()
            x_copies = []
            for k in range(1, NY):
                block = protos.at[x * NY + near_y[k]]
                for side, d in enumerate((1, 3)):
                    x_copies.append(
                        remote(block, block, es.at[k - 1, side], er.at[k - 1, side], device(xs[d], y, z, core))
                    )
        part = row_sums(col_factor)
        if step == ITERS - 1:
            last_col = jnp.where(core == 0, col_factor[:4], col_factor[4:]) * TOTAL_PROTOS
            col_last[yl] = last_col
            for k in range(4):
                last_own[k] = part[2 * k:2 * k + 2].astype(BF16)
            copies = [
                remote(last_own.at[py - NY * lax.div(py, NY)], last_in.at[i], ls.at[i], lr.at[i], peer)
                for i, (py, peer) in enumerate(last_peers)
            ]
            k_copies = [
                remote(col_last.at[yl], col_last.at[yl], ks.at[k - 1], kr.at[k - 1],
                       device(x, yh * NY + near_y[k], z, core))
                for k in range(1, NY)
            ]
            mine_sum = last_own[yl].astype(F32)
            mate_sum = jnp.zeros((2, BLOCK), F32)
            for i, copy in enumerate(copies):
                copy.wait_recv()
                if i < 7:
                    mine_sum = mine_sum + last_in[i].astype(F32)
                else:
                    mate_sum = mate_sum + last_in[i].astype(F32)
            first = jnp.where(core == 0, mine_sum, mate_sum)
            second = jnp.where(core == 0, mate_sum, mine_sum)
            part = jnp.concatenate([first, second], axis=0)
            copies = start(part, lastz_own, lastz_in, lzs, lzr, z_peers)
            for copy in f_copies:
                copy.wait_recv()
            for copy in k_copies:
                copy.wait_recv()
            for b in range(NX * NY):
                scores = lax.dot_general(
                    own_feat[...], unit_rows(protos[b]), NT, preferred_element_type=F32
                )
                factor = col_last[b % NY, b // NY:b // NY + 1, :]
                scaled_ref[:, b * BLOCK:(b + 1) * BLOCK] = jnp.exp(20.0 * scores) * factor
            for copy in sent[:-len(copies)]:
                copy.wait_send()
            row_ref[...] = 1.0 / finish(part, lastz_in, copies)
            for copy in copies:
                copy.wait_send()
            break
        copies = start(part, ring_own.at[step], ring_in.at[step], ys.at[step], yr.at[step], ring_peers)
        far_copies = []
        if step:
            far_copies = [
                remote(ring_own.at[step], far_in.at[i], ds.at[i], dr.at[i], peer)
                for i, peer in enumerate(far_peers)
            ]
        part = finish(part, ring_in.at[step], copies)
        peers = z_peers[1:] if step else z_peers
        copies = start(part, z_own.at[step], z_in.at[step], zs.at[step], zr.at[step], peers)
        if step == 0:
            block = protos.at[batch]
            y_copies = [
                remote(block, block, bs.at[k - 1], br.at[k - 1], device(x, yh * NY + near_y[k], z, core))
                for k in range(1, NY)
            ]
        else:
            f_copies = []
            for k in range(1, NY):
                for side, (source, d) in enumerate(((xs[3], 1), (xs[1], 3))):
                    x_copies[2 * (k - 1) + side].wait_recv()
                    piece = protos.at[source * NY + near_y[k], pl.ds(side * half, half)]
                    f_copies.append(
                        remote(piece, piece, hs.at[k - 1, side], hr.at[k - 1, side], device(xs[d], y, z, core))
                    )
        part = finish(part, z_in.at[step], copies)
        row_factor = 1.0 / finish(part, far_in, far_copies)


def scale_rows(scaled_ref, row_ref, out_ref, rounded, sems):
    copies = []
    for k in range(ROWS // BLOCK):
        column = jnp.broadcast_to(row_ref[k:k + 1, :], (BLOCK, BLOCK)).T
        for first in range(0, BLOCK, PIECE):
            rows = pl.ds(k * BLOCK + first, PIECE)
            factor = jnp.concatenate([column[first:first + PIECE]] * (COLS // BLOCK), axis=1)
            rounded[rows, :] = (scaled_ref[rows, :] * factor).astype(BF16)
            copies.append(
                pltpu.make_async_copy(rounded.at[rows], out_ref.at[rows], sems.at[len(copies)])
            )
            copies[-1].start()
    for copy in copies:
        copy.wait()


def local(features, prototypes):
    vmem = pl.BlockSpec(memory_space=pltpu.VMEM)
    hbm = pl.BlockSpec(memory_space=pltpu.HBM)
    dma = pltpu.SemaphoreType.DMA
    early = ITERS - 1
    scaled, rows = pl.pallas_call(
        kernel,
        out_shape=(
            jax.ShapeDtypeStruct((ROWS, COLS), F32),
            jax.ShapeDtypeStruct((4, BLOCK), F32),
        ),
        in_specs=[hbm, hbm],
        out_specs=(vmem, vmem),
        scratch_shapes=[
            pltpu.VMEM((ROWS, DEPTH), BF16),
            pltpu.VMEM((ROWS, DEPTH), BF16),
            pltpu.VMEM((NY, HALF, DEPTH), BF16),
            pltpu.VMEM((TILE, DEPTH), BF16),
            pltpu.VMEM((NX * NY, BLOCK, DEPTH), BF16),
            pltpu.VMEM((NX, BLOCK, DEPTH), BF16),
            pltpu.VMEM((TILE, DEPTH), BF16),
            pltpu.VMEM((TILE, TILE), BF16),
            pltpu.VMEM((TILE, TILE), BF16),
            pltpu.VMEM((ITERS, 8, BLOCK), BF16),
            pltpu.VMEM((ITERS, 7, 8, BLOCK), BF16),
            pltpu.VMEM((early, 8, BLOCK), BF16),
            pltpu.VMEM((early, 7, 8, BLOCK), BF16),
            pltpu.VMEM((early, 8, BLOCK), BF16),
            pltpu.VMEM((early, 11, 8, BLOCK), BF16),
            pltpu.VMEM((NY, 2, BLOCK), BF16),
            pltpu.VMEM((15, 2, BLOCK), BF16),
            pltpu.VMEM((4, BLOCK), BF16),
            pltpu.VMEM((11, 4, BLOCK), BF16),
            pltpu.VMEM((NY, NX, BLOCK), F32),
            dma((6,)), dma((6,)), dma((3,)), dma((3,)), dma((4,)), dma((4,)),
            dma((ITERS, 7)), dma((ITERS, 7)), dma((early, 7)), dma((early, 7)),
            dma((early, 11)), dma((early, 11)), dma((15,)), dma((15,)), dma((11,)), dma((11,)),
            dma((3,)), dma((3,)), dma((3, 2)), dma((3, 2)), dma((3, 2)), dma((3, 2)), dma((3,)), dma((3,)),
            dma((2,)), pltpu.SemaphoreType.REGULAR, pltpu.SemaphoreType.REGULAR,
            pltpu.VMEM((8, TILE), F32),
            pltpu.VMEM((8, 8, BLOCK), BF16), dma((8,)), dma((8,)),
        ],
        compiler_params=pltpu.CompilerParams(
            collective_id=0, has_side_effects=True, vmem_limit_bytes=24 << 20
        ),
    )(*(pltpu.with_memory_space_constraint(array, pltpu.HBM) for array in (features, prototypes)))
    pieces = ROWS // PIECE
    return pl.pallas_call(
        scale_rows,
        out_shape=jax.ShapeDtypeStruct((ROWS, COLS), BF16),
        in_specs=[vmem, vmem],
        out_specs=pl.BlockSpec(memory_space=pltpu.HBM),
        scratch_shapes=[pltpu.VMEM((ROWS, COLS), BF16), dma((pieces,))],
        compiler_params=pltpu.CompilerParams(vmem_limit_bytes=16 << 20),
    )(scaled, rows)


def solution(mesh):
    in_specs = (P("batch", None), P(("proto", "batch"), None))
    out_specs = P("batch", "proto")
    return jax.shard_map(local, mesh=mesh, in_specs=in_specs, out_specs=out_specs, check_vma=False)
```
